32 devices in a mesh: space: 4 (over z), energy: 8 (over y, x, core).
Axes of the slice: x: 2, y: 2, z: 4, core: 2. Of those that a mesh axis runs over, the one named last changes fastest.
Arguments:
- retain: float32 [8, 8], P('space', 'energy'), may hold values from 0.12 to 0.89
- hopping: float32 [8, 8, 2, 128, 128], P('space', 'energy'), may hold values from -0.125 to 0.125
- source: float32 [8, 8, 2, 128, 128], P('space', 'energy'), may hold values from -0.9 to 0.9
- screened: float32 [8, 8, 2, 16384], P('space', None, None, 'energy'), may hold values from -2 to 2
Outputs:
- greens: float32 [8, 8, 2, 128, 128], P('space', 'energy')
- self_energy: float32 [8, 8, 2, 16384], P('space', None, None, 'energy')
The draws below stay inside these ranges and needn't reach their ends.
All inputs are finite; a program needn't handle non-finite values.
Results may differ from the reference program's by a relative error of at most 0.0001.
Values sent between devices are 32-bit elements; how exact they have to be, the bound alone decides.
A program may use at most 64 MiB of HBM per device.

```python
import math
import jax
import jax.numpy as jnp
from jax import lax

M = 128
SLAB_COUNT = 8
ENERGY_COUNT = 8


def draw_retain(key, part):
    root_random_key = jax.random.fold_in(key, 11)
    wobble_random_key, quick_random_key, spike_random_key, damping_random_key = jax.random.split(root_random_key, 4)
    jitter = jnp.exp(jax.random.uniform(wobble_random_key, (SLAB_COUNT, ENERGY_COUNT), jnp.float32, math.log(0.5), math.log(2.0)))
    fast_share = 0.5
    fast_mask = jax.random.uniform(quick_random_key, (1, ENERGY_COUNT), jnp.float32) < fast_share
    slow_rate = jnp.exp(-0.5 * jitter / SLAB_COUNT)
    fast_rate = jnp.exp(-0.8 * jitter)
    noise_amplitude = jnp.where(fast_mask, fast_rate, slow_rate)
    spike_slab_list = jax.random.randint(spike_random_key, (2,), 0, SLAB_COUNT)
    slab_ordinals = jnp.arange(SLAB_COUNT)[:, None]
    spike_slab_mask = (slab_ordinals == spike_slab_list[0]) | (slab_ordinals == spike_slab_list[1])
    spike_loss_factor = jax.random.uniform(damping_random_key, (SLAB_COUNT, ENERGY_COUNT), jnp.float32, 0.5, 0.8)
    noise_amplitude = jnp.where(spike_slab_mask, noise_amplitude * jnp.sqrt(spike_loss_factor), noise_amplitude)
    return (noise_amplitude / 1.125).astype(jnp.float32)


def level_of(stream_key, dims, shards, low, high):
    factor_of = 1.0
    for dim, shards_of in shards:
        heights = jax.random.uniform(jax.random.fold_in(jax.random.fold_in(stream_key, 6), dim), (shards_of,), jnp.float32, low / len(shards), high / len(shards))
        factor_of = factor_of * jnp.repeat(jnp.exp(heights), dims[dim] // shards_of).reshape((-1,) + (1,) * (len(dims) - 1 - dim))
    return factor_of


def noise(rng, extent, deviation, limit, pieces=(), kind=jnp.bfloat16):
    drawn = deviation * jax.random.normal(rng, extent, jnp.float32)
    if pieces:
        drawn = drawn * level_of(rng, extent, pieces, -0.22, 0.18)
    return jnp.clip(drawn, -limit, limit).astype(kind)


def setup_inputs(seed: int = 0) -> dict:
    streams_of = jax.random.split(jax.random.key(seed), 5)
    return {
        "retain": draw_retain(jax.random.fold_in(streams_of[4], 71), 0),
        "hopping": noise(streams_of[1], (SLAB_COUNT, ENERGY_COUNT, 2, M, M), (16 * M) ** -0.5, 0.125, ((0, 4), (1, 8)), jnp.float32),
        "source": noise(streams_of[2], (SLAB_COUNT, ENERGY_COUNT, 2, M, M), 0.15, 0.9, ((0, 4), (1, 8)), jnp.float32),
        "screened": noise(streams_of[3], (SLAB_COUNT, ENERGY_COUNT, 2, M * M), ENERGY_COUNT ** -0.5, 2.0, ((0, 4), (3, 8)), jnp.float32),
    }


EXACT_PRECISION = lax.Precision.HIGHEST


def build_coupler(retain_slab, hop_slab):
    size = hop_slab.shape[-1]
    diagonal_ones = jnp.eye(size, dtype=jnp.float32)
    factor = retain_slab[:, None, None]
    return jnp.stack([factor * (diagonal_ones + hop_slab[:, 0]), factor * hop_slab[:, 1]], axis=1)


def complex_product(left_matrix, right_matrix):
    real_component = jnp.einsum("eij,ejk->eik", left_matrix[:, 0], right_matrix[:, 0], precision=EXACT_PRECISION) - jnp.einsum("eij,ejk->eik", left_matrix[:, 1], right_matrix[:, 1], precision=EXACT_PRECISION)
    imaginary_component = jnp.einsum("eij,ejk->eik", left_matrix[:, 0], right_matrix[:, 1], precision=EXACT_PRECISION) + jnp.einsum("eij,ejk->eik", left_matrix[:, 1], right_matrix[:, 0], precision=EXACT_PRECISION)
    return jnp.stack([real_component, imaginary_component], axis=1)


def times_dagger(left_matrix, right_matrix):
    real_component = jnp.einsum("eij,ekj->eik", left_matrix[:, 0], right_matrix[:, 0], precision=EXACT_PRECISION) + jnp.einsum("eij,ekj->eik", left_matrix[:, 1], right_matrix[:, 1], precision=EXACT_PRECISION)
    imaginary_component = jnp.einsum("eij,ekj->eik", left_matrix[:, 1], right_matrix[:, 0], precision=EXACT_PRECISION) - jnp.einsum("eij,ekj->eik", left_matrix[:, 0], right_matrix[:, 1], precision=EXACT_PRECISION)
    return jnp.stack([real_component, imaginary_component], axis=1)


def sandwich(coupler, middle):
    return times_dagger(complex_product(coupler, middle), coupler)


def reference(retain, hopping, source, screened):
    def slab_step(entering, slab_data):
        retain_slab, hop_slab, fresh_source = slab_data
        coupler = build_coupler(retain_slab, hop_slab)
        leaving = sandwich(coupler, entering) + fresh_source
        return leaving, leaving

    start_block = jnp.zeros((ENERGY_COUNT, 2, M, M), jnp.float32)
    _, greens = lax.scan(slab_step, start_block, (retain, hopping, source))
    pair_blocks = greens.reshape(SLAB_COUNT, ENERGY_COUNT, 2, M * M)

    def convolve(slab_data):
        green_slab, screen_slab = slab_data
        padded = jnp.concatenate([jnp.zeros_like(green_slab), green_slab], axis=0)

        def add_term(boson_index, running_sum):
            shifted = lax.dynamic_slice_in_dim(padded, (ENERGY_COUNT - boson_index).astype(jnp.int32), ENERGY_COUNT, 0)
            weight = lax.dynamic_slice_in_dim(screen_slab, boson_index.astype(jnp.int32), 1, 0)
            real_component = shifted[:, 0] * weight[:, 0] - shifted[:, 1] * weight[:, 1]
            imaginary_component = shifted[:, 0] * weight[:, 1] + shifted[:, 1] * weight[:, 0]
            return running_sum + jnp.stack([real_component, imaginary_component], axis=1)

        return lax.fori_loop(0, ENERGY_COUNT, add_term, jnp.zeros_like(green_slab))

    self_energy = lax.map(convolve, (pair_blocks, screened))
    return greens, self_energy
```

```python
import functools

import jax
import jax.numpy as jnp
from jax import lax
from jax.experimental import pallas as pl
from jax.experimental.pallas import tpu as pltpu
from jax.sharding import PartitionSpec as P

MESH = pl.DeviceIdType.MESH
F32 = jnp.float32
BF16 = jnp.bfloat16
CHUNKS = 2
NN = (((1,), (0,)), ((), ()))
NT = (((1,), (1,)), ((), ()))


def split(value):
    high = value.astype(BF16)
    return high, (value - high.astype(F32)).astype(BF16)


def product(left, right, dims=NN):
    dot = functools.partial(lax.dot_general, dimension_numbers=dims, preferred_element_type=F32)
    (lh, ll), (rh, rl) = left, right
    return dot(lh, rh) + (dot(lh, rl) + dot(ll, rh))


def left_form(real, imag):
    return jnp.concatenate(
        [jnp.concatenate([real, -imag], 1), jnp.concatenate([imag, real], 1)], 0
    )


def dagger_form(real, imag):
    return jnp.concatenate(
        [jnp.concatenate([real, imag], 1), jnp.concatenate([-imag, real], 1)], 0
    )


def kernel(
    retain, hop_hbm, src_hbm, scr_hbm, out_g, out_se,
    hop, src, scr, lefts, rights, bases, g, stage, entering, landed,
    load_sem, chain_send, chain_recv, swap_send, swap_recv, out_sem,
):
    slabs, _, size, _ = hop.shape
    energies, rows = stage.shape[1], stage.shape[3]
    space, energy = lax.axis_index("space"), lax.axis_index("energy")
    stages = lax.axis_size("space")
    piece = size // CHUNKS

    loads = [
        pltpu.make_async_copy(hop_hbm.at[:, 0], hop, load_sem.at[0]),
        pltpu.make_async_copy(src_hbm.at[:, 0], src, load_sem.at[1]),
        pltpu.make_async_copy(scr_hbm, scr, load_sem.at[2]),
    ]
    for load in loads:
        load.start()

    barrier = pltpu.get_barrier_semaphore()
    for step in range(1, energies):
        pl.semaphore_signal(
            barrier, inc=1, device_id=(space, lax.rem(energy + step, energies)), device_id_type=MESH
        )

    @pl.when(space > 0)
    def _():
        pl.semaphore_signal(barrier, inc=1, device_id=(space - 1, energy), device_id_type=MESH)

    loads[0].wait()
    loads[1].wait()

    eye = (
        lax.broadcasted_iota(jnp.int32, (size, size), 0)
        == lax.broadcasted_iota(jnp.int32, (size, size), 1)
    ).astype(F32)
    couplers = []
    for j in range(slabs):
        factor = retain[j, 0]
        couplers.append((factor * (eye + hop[j, 0]), factor * hop[j, 1]))

    def sandwich(left, right, real, imag):
        turned = product(split(jnp.concatenate([real, imag], 1)), right, NT)
        return product(left, split(jnp.concatenate([turned[:, :size], turned[:, size:]], 0)))

    base = jnp.concatenate([src[0, 0], src[0, 1]], 0)
    bases[0] = base
    step_lefts = [None]
    for j in range(1, slabs):
        step_left = split(left_form(*couplers[j]))
        step_right = split(dagger_form(*couplers[j]))
        step_lefts.append(step_left)
        base = sandwich(step_left, step_right, base[:size], base[size:]) + jnp.concatenate(
            [src[j, 0], src[j, 1]], 0
        )
        bases[j] = base

    def chain(c):
        part = pl.ds(c * piece, piece)
        return pltpu.make_async_remote_copy(
            src_ref=g.at[slabs - 1, :, part],
            dst_ref=entering.at[:, part],
            send_sem=chain_send.at[c],
            recv_sem=chain_recv.at[c],
            device_id=(space + 1, energy),
            device_id_type=MESH,
        )

    def swap(j, step):
        peer = lax.rem(energy + step, energies)
        return pltpu.make_async_remote_copy(
            src_ref=stage.at[j, peer],
            dst_ref=landed.at[j, energy],
            send_sem=swap_send.at[j, step],
            recv_sem=swap_recv.at[j, step],
            device_id=(space, peer),
            device_id_type=MESH,
        )

    def put(j, block):
        g[j, 0] = block[:size]
        g[j, 1] = block[size:]

    def spread(j):
        for q in range(energies):
            for part in range(2):
                stage[j, q, part] = g[j, part, q * rows : (q + 1) * rows]
        for step in range(1, energies):
            swap(j, step).start()
        pltpu.make_async_copy(g.at[j], out_g.at[j, 0], out_sem.at[j]).start()

    pl.semaphore_wait(barrier, energies - 1 + (space < stages - 1).astype(jnp.int32))

    last = slabs - 1

    @pl.when(space == 0)
    def _():
        put(last, bases[last])

        @pl.when(space < stages - 1)
        def _():
            for c in range(CHUNKS):
                chain(c).start()

        spread(last)
        for j in range(last - 1, -1, -1):
            put(j, bases[j])
            spread(j)

    @pl.when(space > 0)
    def _():
        real, imag = couplers[0]
        for j in range(slabs):
            if j > 0:
                both = product(step_lefts[j], split(jnp.concatenate([real, imag], 0)))
                real, imag = both[:size], both[size:]
            for ref, form in ((lefts, left_form), (rights, dagger_form)):
                high, low = split(form(real, imag))
                ref[j, 0] = high
                ref[j, 1] = low

        turned = []
        for c in range(CHUNKS):
            chain(c).wait_recv()
            lines = slice(c * piece, (c + 1) * piece)
            arrived = split(jnp.concatenate([entering[0, lines], entering[1, lines]], 1))
            turned.append(product(arrived, (rights[last, 0], rights[last, 1]), NT))
        turned = jnp.concatenate(turned, 0)
        inner = split(jnp.concatenate([turned[:, :size], turned[:, size:]], 0))
        put(last, product((lefts[last, 0], lefts[last, 1]), inner) + bases[last])

        @pl.when(space < stages - 1)
        def _():
            for c in range(CHUNKS):
                chain(c).start()

        spread(last)
        for j in range(last - 1, -1, -1):
            put(
                j,
                sandwich(
                    (lefts[j, 0], lefts[j, 1]),
                    (rights[j, 0], rights[j, 1]),
                    entering[0],
                    entering[1],
                )
                + bases[j],
            )
            spread(j)

    loads[2].wait()
    for j in range(last, -1, -1):
        landed[j, energy] = stage[j, energy]
        for step in range(1, energies):
            swap(j, step).wait_recv()
        for e in range(energies):
            real = jnp.zeros((rows, size), F32)
            imag = jnp.zeros((rows, size), F32)
            for w in range(e + 1):
                gr, gi = landed[j, e - w, 0], landed[j, e - w, 1]
                sr, si = scr[j, w, 0], scr[j, w, 1]
                real = real + (gr * sr - gi * si)
                imag = imag + (gr * si + gi * sr)
            out_se[j, e, 0] = real
            out_se[j, e, 1] = imag

    for j in range(slabs):
        for step in range(1, energies):
            swap(j, step).wait_send()
        pltpu.make_async_copy(g.at[j], out_g.at[j, 0], out_sem.at[j]).wait()

    @pl.when(space < stages - 1)
    def _():
        for c in range(CHUNKS):
            chain(c).wait_send()


def body(retain, hopping, source, screened):
    slabs, _, _, size, _ = hopping.shape
    energies = screened.shape[1]
    rows = screened.shape[3] // size
    tall = screened.reshape(slabs, energies, 2, rows, size)
    any_spec = pl.BlockSpec(memory_space=pl.ANY)
    vmem = pltpu.VMEM
    greens, self_energy = pl.pallas_call(
        kernel,
        out_shape=(
            jax.ShapeDtypeStruct(source.shape, F32),
            jax.ShapeDtypeStruct(tall.shape, F32),
        ),
        in_specs=[pl.BlockSpec(memory_space=pltpu.SMEM), any_spec, any_spec, any_spec],
        out_specs=(any_spec, pl.BlockSpec(memory_space=pltpu.VMEM)),
        scratch_shapes=[
            vmem((slabs, 2, size, size), F32),
            vmem((slabs, 2, size, size), F32),
            vmem(tall.shape, F32),
            vmem((slabs, 2, 2 * size, 2 * size), BF16),
            vmem((slabs, 2, 2 * size, 2 * size), BF16),
            vmem((slabs, 2 * size, size), F32),
            vmem((slabs, 2, size, size), F32),
            vmem((slabs, energies, 2, rows, size), F32),
            vmem((2, size, size), F32),
            vmem((slabs, energies, 2, rows, size), F32),
            pltpu.SemaphoreType.DMA((3,)),
            pltpu.SemaphoreType.DMA((CHUNKS,)),
            pltpu.SemaphoreType.DMA((CHUNKS,)),
            pltpu.SemaphoreType.DMA((slabs, energies)),
            pltpu.SemaphoreType.DMA((slabs, energies)),
            pltpu.SemaphoreType.DMA((slabs,)),
        ],
        compiler_params=pltpu.CompilerParams(collective_id=0, has_side_effects=True),
    )(retain, hopping, source, tall)
    return greens, self_energy.reshape(screened.shape)


def solution(mesh):
    placed = (
        P("space", "energy"),
        P("space", "energy", None, None, None),
        P("space", "energy", None, None, None),
        P("space", None, None, "energy"),
    )
    return jax.shard_map(
        body,
        mesh=mesh,
        in_specs=placed,
        out_specs=(P("space", "energy", None, None, None), P("space", None, None, "energy")),
        check_vma=False,
    )
```

```python
import functools

import jax
import jax.numpy as jnp
from jax import lax
from jax.experimental import pallas as pl
from jax.experimental.pallas import tpu as pltpu
from jax.sharding import PartitionSpec as P

MESH = pl.DeviceIdType.MESH
F32 = jnp.float32
BF16 = jnp.bfloat16
CHUNKS = 2
NN = (((1,), (0,)), ((), ()))
NT = (((1,), (1,)), ((), ()))


def split(value):
    high = value.astype(BF16)
    return high, (value - high.astype(F32)).astype(BF16)


def product(left, right, dims=NN):
    dot = functools.partial(lax.dot_general, dimension_numbers=dims, preferred_element_type=F32)
    (lh, ll), (rh, rl) = left, right
    return dot(lh, rh) + (dot(lh, rl) + dot(ll, rh))


def left_form(real, imag):
    return jnp.concatenate(
        [jnp.concatenate([real, -imag], 1), jnp.concatenate([imag, real], 1)], 0
    )


def dagger_form(real, imag):
    return jnp.concatenate(
        [jnp.concatenate([real, imag], 1), jnp.concatenate([-imag, real], 1)], 0
    )


def kernel(
    retain_hbm, hop_hbm, src_hbm, scr_hbm, g, out_se,
    retain, hop, src, scr, lefts, rights, bases, stage, entering, landed,
    load_sem, chain_send, chain_recv, swap_send, swap_recv,
):
    slabs, _, size, _ = hop.shape
    energies, rows = stage.shape[1], stage.shape[3]
    space, energy = lax.axis_index("space"), lax.axis_index("energy")
    stages = lax.axis_size("space")
    piece = size // CHUNKS

    loads = [
        pltpu.make_async_copy(hop_hbm.at[:, 0], hop, load_sem.at[0]),
        pltpu.make_async_copy(src_hbm.at[:, 0], src, load_sem.at[1]),
        pltpu.make_async_copy(scr_hbm, scr, load_sem.at[2]),
        pltpu.make_async_copy(retain_hbm, retain, load_sem.at[3]),
    ]
    for load in loads:
        load.start()

    barrier = pltpu.get_barrier_semaphore()
    for step in range(1, energies):
        pl.semaphore_signal(
            barrier, inc=1, device_id=(space, lax.rem(energy + step, energies)), device_id_type=MESH
        )

    @pl.when(space > 0)
    def _():
        pl.semaphore_signal(barrier, inc=1, device_id=(space - 1, energy), device_id_type=MESH)

    loads[3].wait()
    loads[0].wait()
    loads[1].wait()

    eye = (
        lax.broadcasted_iota(jnp.int32, (size, size), 0)
        == lax.broadcasted_iota(jnp.int32, (size, size), 1)
    ).astype(F32)
    couplers = []
    for j in range(slabs):
        factor = retain[j]
        couplers.append((factor * (eye + hop[j, 0]), factor * hop[j, 1]))

    def sandwich(left, right, real, imag):
        turned = product(split(jnp.concatenate([real, imag], 1)), right, NT)
        return product(left, split(jnp.concatenate([turned[:, :size], turned[:, size:]], 0)))

    base = jnp.concatenate([src[0, 0], src[0, 1]], 0)
    bases[0] = base
    step_lefts = [None]
    for j in range(1, slabs):
        step_left = split(left_form(*couplers[j]))
        step_right = split(dagger_form(*couplers[j]))
        step_lefts.append(step_left)
        base = sandwich(step_left, step_right, base[:size], base[size:]) + jnp.concatenate(
            [src[j, 0], src[j, 1]], 0
        )
        bases[j] = base

    def chain(c):
        part = pl.ds(c * piece, piece)
        return pltpu.make_async_remote_copy(
            src_ref=g.at[slabs - 1, :, part],
            dst_ref=entering.at[:, part],
            send_sem=chain_send.at[c],
            recv_sem=chain_recv.at[c],
            device_id=(space + 1, energy),
            device_id_type=MESH,
        )

    def swap(j, step):
        peer = lax.rem(energy + step, energies)
        return pltpu.make_async_remote_copy(
            src_ref=stage.at[j, peer],
            dst_ref=landed.at[j, energy],
            send_sem=swap_send.at[j, step],
            recv_sem=swap_recv.at[j, step],
            device_id=(space, peer),
            device_id_type=MESH,
        )

    def put(j, block):
        g[j, 0] = block[:size]
        g[j, 1] = block[size:]

    def spread(j):
        for q in range(energies):
            for part in range(2):
                stage[j, q, part] = g[j, part, q * rows : (q + 1) * rows]
        for step in range(1, energies):
            swap(j, step).start()

    pl.semaphore_wait(barrier, energies - 1 + (space < stages - 1).astype(jnp.int32))

    last = slabs - 1

    @pl.when(space == 0)
    def _():
        put(last, bases[last])

        @pl.when(space < stages - 1)
        def _():
            for c in range(CHUNKS):
                chain(c).start()

        spread(last)
        for j in range(last - 1, -1, -1):
            put(j, bases[j])
            spread(j)

    @pl.when(space > 0)
    def _():
        real, imag = couplers[0]
        for j in range(slabs):
            if j > 0:
                both = product(step_lefts[j], split(jnp.concatenate([real, imag], 0)))
                real, imag = both[:size], both[size:]
            for ref, form in ((lefts, left_form), (rights, dagger_form)):
                high, low = split(form(real, imag))
                ref[j, 0] = high
                ref[j, 1] = low

        turned = []
        for c in range(CHUNKS):
            chain(c).wait_recv()
            lines = slice(c * piece, (c + 1) * piece)
            arrived = split(jnp.concatenate([entering[0, lines], entering[1, lines]], 1))
            turned.append(product(arrived, (rights[last, 0], rights[last, 1]), NT))
        turned = jnp.concatenate(turned, 0)
        inner = split(jnp.concatenate([turned[:, :size], turned[:, size:]], 0))
        put(last, product((lefts[last, 0], lefts[last, 1]), inner) + bases[last])

        @pl.when(space < stages - 1)
        def _():
            for c in range(CHUNKS):
                chain(c).start()

        spread(last)
        for j in range(last - 1, -1, -1):
            put(
                j,
                sandwich(
                    (lefts[j, 0], lefts[j, 1]),
                    (rights[j, 0], rights[j, 1]),
                    entering[0],
                    entering[1],
                )
                + bases[j],
            )
            spread(j)

    def lanes(part):
        return pl.ds(part, rows, stride=2)

    loads[2].wait()
    for j in range(last, -1, -1):
        landed[j, energy] = stage[j, energy]
        for step in range(1, energies):
            swap(j, step).wait_recv()
        for e in range(energies):
            real = jnp.zeros((rows, size), F32)
            imag = jnp.zeros((rows, size), F32)
            for w in range(e + 1):
                gr, gi = landed[j, e - w, 0], landed[j, e - w, 1]
                sr, si = scr[j, w, lanes(0)], scr[j, w, lanes(1)]
                real = real + (gr * sr - gi * si)
                imag = imag + (gr * si + gi * sr)
            out_se[j, e, lanes(0)] = real
            out_se[j, e, lanes(1)] = imag

    for j in range(slabs):
        for step in range(1, energies):
            swap(j, step).wait_send()

    @pl.when(space < stages - 1)
    def _():
        for c in range(CHUNKS):
            chain(c).wait_send()


def write_out(g, se, out_g, out_se, sems):
    copies = [
        pltpu.make_async_copy(g, out_g.at[:, 0], sems.at[0]),
        pltpu.make_async_copy(se, out_se, sems.at[1]),
    ]
    for copy in copies:
        copy.start()
    for copy in copies:
        copy.wait()


def body(retain, hopping, source, screened):
    slabs, _, _, size, _ = hopping.shape
    energies = screened.shape[1]
    rows = screened.shape[3] // size
    woven = (
        screened.reshape(slabs, energies, 2, rows, size)
        .transpose(0, 1, 3, 2, 4)
        .reshape(slabs, energies, 2 * rows, size)
    )
    any_spec = pl.BlockSpec(memory_space=pl.ANY)
    vmem_spec = pl.BlockSpec(memory_space=pltpu.VMEM)
    vmem = pltpu.VMEM
    greens, self_energy = pl.pallas_call(
        kernel,
        out_shape=(vmem((slabs, 2, size, size), F32), vmem(woven.shape, F32)),
        in_specs=[pl.BlockSpec(memory_space=pltpu.HBM)] * 4,
        out_specs=(vmem_spec, vmem_spec),
        scratch_shapes=[
            pltpu.SMEM((slabs,), F32),
            vmem((slabs, 2, size, size), F32),
            vmem((slabs, 2, size, size), F32),
            vmem(woven.shape, F32),
            vmem((slabs, 2, 2 * size, 2 * size), BF16),
            vmem((slabs, 2, 2 * size, 2 * size), BF16),
            vmem((slabs, 2 * size, size), F32),
            vmem((slabs, energies, 2, rows, size), F32),
            vmem((2, size, size), F32),
            vmem((slabs, energies, 2, rows, size), F32),
            pltpu.SemaphoreType.DMA((4,)),
            pltpu.SemaphoreType.DMA((CHUNKS,)),
            pltpu.SemaphoreType.DMA((CHUNKS,)),
            pltpu.SemaphoreType.DMA((slabs, energies)),
            pltpu.SemaphoreType.DMA((slabs, energies)),
        ],
        compiler_params=pltpu.CompilerParams(
            collective_id=0, has_side_effects=True
        ),
    )(retain.reshape(slabs), hopping, source, woven)
    greens, self_energy = pl.pallas_call(
        write_out,
        out_shape=(
            jax.ShapeDtypeStruct(source.shape, F32),
            jax.ShapeDtypeStruct(woven.shape, F32),
        ),
        in_specs=[vmem_spec, vmem_spec],
        out_specs=(any_spec, any_spec),
        scratch_shapes=[pltpu.SemaphoreType.DMA((2,))],
        compiler_params=pltpu.CompilerParams(vmem_limit_bytes=4 << 20),
    )(greens, self_energy)
    return greens, (
        self_energy.reshape(slabs, energies, rows, 2, size)
        .transpose(0, 1, 3, 2, 4)
        .reshape(screened.shape)
    )


def solution(mesh):
    placed = (
        P("space", "energy"),
        P("space", "energy", None, None, None),
        P("space", "energy", None, None, None),
        P("space", None, None, "energy"),
    )
    return jax.shard_map(
        body,
        mesh=mesh,
        in_specs=placed,
        out_specs=(P("space", "energy", None, None, None), P("space", None, None, "energy")),
        check_vma=False,
    )
```

```python
import functools

import jax
import jax.numpy as jnp
from jax import lax
from jax.experimental import pallas as pl
from jax.experimental.pallas import tpu as pltpu
from jax.sharding import PartitionSpec as P

MESH = pl.DeviceIdType.MESH
F32 = jnp.float32
BF16 = jnp.bfloat16
CHUNKS = 4
NN = (((1,), (0,)), ((), ()))
NT = (((1,), (1,)), ((), ()))


def split(value):
    high = value.astype(BF16)
    return high, (value - high.astype(F32)).astype(BF16)


def product(left, right, dims=NN):
    dot = functools.partial(lax.dot_general, dimension_numbers=dims, preferred_element_type=F32)
    (lh, ll), (rh, rl) = left, right
    return dot(lh, rh) + (dot(lh, rl) + dot(ll, rh))


def left_form(real, imag):
    return jnp.concatenate(
        [jnp.concatenate([real, -imag], 1), jnp.concatenate([imag, real], 1)], 0
    )


def dagger_form(real, imag):
    return jnp.concatenate(
        [jnp.concatenate([real, imag], 1), jnp.concatenate([-imag, real], 1)], 0
    )


def kernel(
    retain_hbm, hop_hbm, src_hbm, scr_hbm, g, out_se,
    retain, hop, src, scr, lefts, rights, bases, stage, entering, landed, own_map, early,
    load_sem, chain_send, chain_recv, swap_send, swap_recv, early_send, early_recv,
):
    slabs, _, size, _ = hop.shape
    energies, rows = stage.shape[1], stage.shape[3]
    space, energy = lax.axis_index("space"), lax.axis_index("energy")
    stages = lax.axis_size("space")
    piece = size // CHUNKS
    relays = (space % 2 == 0) & (space > 0) & (space < stages - 1)
    paired = (space % 2 == 1) & (space > 1)

    loads = [
        pltpu.make_async_copy(hop_hbm.at[:, 0], hop, load_sem.at[0]),
        pltpu.make_async_copy(src_hbm.at[:, 0], src, load_sem.at[1]),
        pltpu.make_async_copy(scr_hbm, scr, load_sem.at[2]),
        pltpu.make_async_copy(retain_hbm, retain, load_sem.at[3]),
    ]
    for load in loads:
        load.start()

    barrier = pltpu.get_barrier_semaphore()
    for step in range(1, energies):
        pl.semaphore_signal(
            barrier, inc=1, device_id=(space, lax.rem(energy + step, energies)), device_id_type=MESH
        )

    @pl.when(space > 0)
    def _():
        pl.semaphore_signal(barrier, inc=1, device_id=(space - 1, energy), device_id_type=MESH)

    loads[3].wait()
    loads[0].wait()
    loads[1].wait()

    eye = (
        lax.broadcasted_iota(jnp.int32, (size, size), 0)
        == lax.broadcasted_iota(jnp.int32, (size, size), 1)
    ).astype(F32)
    couplers = []
    for j in range(slabs):
        factor = retain[j]
        couplers.append((factor * (eye + hop[j, 0]), factor * hop[j, 1]))

    def sandwich(left, right, real, imag):
        turned = product(split(jnp.concatenate([real, imag], 1)), right, NT)
        return product(left, split(jnp.concatenate([turned[:, :size], turned[:, size:]], 0)))

    base = jnp.concatenate([src[0, 0], src[0, 1]], 0)
    bases[0] = base
    step_lefts = [None]
    for j in range(1, slabs):
        step_left = split(left_form(*couplers[j]))
        step_right = split(dagger_form(*couplers[j]))
        step_lefts.append(step_left)
        base = sandwich(step_left, step_right, base[:size], base[size:]) + jnp.concatenate(
            [src[j, 0], src[j, 1]], 0
        )
        bases[j] = base

    def chain(c, relay=False):
        part = pl.ds(c * piece, piece)
        return pltpu.make_async_remote_copy(
            src_ref=entering.at[:, part] if relay else g.at[slabs - 1, :, part],
            dst_ref=entering.at[:, part],
            send_sem=chain_send.at[c],
            recv_sem=chain_recv.at[c],
            device_id=(space + 1, energy),
            device_id_type=MESH,
        )

    def ahead(i):
        return pltpu.make_async_remote_copy(
            src_ref=bases.at[slabs - 1] if i else own_map,
            dst_ref=early.at[i],
            send_sem=early_send.at[i],
            recv_sem=early_recv.at[i],
            device_id=(space + 1, energy),
            device_id_type=MESH,
        )

    def swap(j, step):
        peer = lax.rem(energy + step, energies)
        return pltpu.make_async_remote_copy(
            src_ref=stage.at[j, peer],
            dst_ref=landed.at[j, energy],
            send_sem=swap_send.at[j, step],
            recv_sem=swap_recv.at[j, step],
            device_id=(space, peer),
            device_id_type=MESH,
        )

    def keep(j, real, imag):
        for ref, form in ((lefts, left_form), (rights, dagger_form)):
            high, low = split(form(real, imag))
            ref[j, 0] = high
            ref[j, 1] = low

    def put(j, block):
        g[j, 0] = block[:size]
        g[j, 1] = block[size:]

    def spread(j):
        for q in range(energies):
            for part in range(2):
                stage[j, q, part] = g[j, part, q * rows : (q + 1) * rows]
        for step in range(1, energies):
            swap(j, step).start()

    pl.semaphore_wait(barrier, energies - 1 + (space < stages - 1).astype(jnp.int32))

    last = slabs - 1

    @pl.when(space == 0)
    def _():
        put(last, bases[last])

        @pl.when(space < stages - 1)
        def _():
            for c in range(CHUNKS):
                chain(c).start()

        spread(last)
        for j in range(last - 1, -1, -1):
            put(j, bases[j])
            spread(j)

    @pl.when(space > 0)
    def _():
        real, imag = couplers[0]
        for j in range(slabs):
            if j > 0:
                both = product(step_lefts[j], split(jnp.concatenate([real, imag], 0)))
                real, imag = both[:size], both[size:]
            keep(j, real, imag)
        own_map[...] = jnp.concatenate([real, imag], 0)

        @pl.when(relays)
        def _():
            ahead(0).start()
            ahead(1).start()

        @pl.when(paired)
        def _():
            ahead(0).wait_recv()
            ahead(1).wait_recv()
            before = split(early[0])
            for j in range(slabs):
                left = lefts[j, 0], lefts[j, 1]
                right = rights[j, 0], rights[j, 1]
                bases[j] = sandwich(left, right, early[1, :size], early[1, size:]) + bases[j]
                both = product(left, before)
                keep(j, both[:size], both[size:])

        turned = []
        for c in range(CHUNKS):
            chain(c).wait_recv()

            @pl.when(relays)
            def _():
                chain(c, True).start()

            lines = slice(c * piece, (c + 1) * piece)
            arrived = split(jnp.concatenate([entering[0, lines], entering[1, lines]], 1))
            turned.append(product(arrived, (rights[last, 0], rights[last, 1]), NT))
        turned = jnp.concatenate(turned, 0)
        inner = split(jnp.concatenate([turned[:, :size], turned[:, size:]], 0))
        put(last, product((lefts[last, 0], lefts[last, 1]), inner) + bases[last])

        @pl.when((space < stages - 1) & (space % 2 == 1))
        def _():
            for c in range(CHUNKS):
                chain(c).start()

        spread(last)
        for j in range(last - 1, -1, -1):
            put(
                j,
                sandwich(
                    (lefts[j, 0], lefts[j, 1]),
                    (rights[j, 0], rights[j, 1]),
                    entering[0],
                    entering[1],
                )
                + bases[j],
            )
            spread(j)

    def lanes(part):
        return pl.ds(part, rows, stride=2)

    loads[2].wait()
    for j in range(last, -1, -1):
        landed[j, energy] = stage[j, energy]
        for step in range(1, energies):
            swap(j, step).wait_recv()
        for e in range(energies):
            real = jnp.zeros((rows, size), F32)
            imag = jnp.zeros((rows, size), F32)
            for w in range(e + 1):
                gr, gi = landed[j, e - w, 0], landed[j, e - w, 1]
                sr, si = scr[j, w, lanes(0)], scr[j, w, lanes(1)]
                real = real + (gr * sr - gi * si)
                imag = imag + (gr * si + gi * sr)
            out_se[j, e, lanes(0)] = real
            out_se[j, e, lanes(1)] = imag

    for j in range(slabs):
        for step in range(1, energies):
            swap(j, step).wait_send()

    @pl.when((space < stages - 1) & jnp.logical_not(relays))
    def _():
        for c in range(CHUNKS):
            chain(c).wait_send()

    @pl.when(relays)
    def _():
        ahead(0).wait_send()
        ahead(1).wait_send()
        for c in range(CHUNKS):
            chain(c, True).wait_send()


def write_out(g, se, out_g, out_se, sems):
    copies = [
        pltpu.make_async_copy(g, out_g.at[:, 0], sems.at[0]),
        pltpu.make_async_copy(se, out_se, sems.at[1]),
    ]
    for copy in copies:
        copy.start()
    for copy in copies:
        copy.wait()


def body(retain, hopping, source, screened):
    slabs, _, _, size, _ = hopping.shape
    energies = screened.shape[1]
    rows = screened.shape[3] // size
    woven = (
        screened.reshape(slabs, energies, 2, rows, size)
        .transpose(0, 1, 3, 2, 4)
        .reshape(slabs, energies, 2 * rows, size)
    )
    any_spec = pl.BlockSpec(memory_space=pl.ANY)
    vmem_spec = pl.BlockSpec(memory_space=pltpu.VMEM)
    vmem = pltpu.VMEM
    greens, self_energy = pl.pallas_call(
        kernel,
        out_shape=(vmem((slabs, 2, size, size), F32), vmem(woven.shape, F32)),
        in_specs=[pl.BlockSpec(memory_space=pltpu.HBM)] * 4,
        out_specs=(vmem_spec, vmem_spec),
        scratch_shapes=[
            pltpu.SMEM((slabs,), F32),
            vmem((slabs, 2, size, size), F32),
            vmem((slabs, 2, size, size), F32),
            vmem(woven.shape, F32),
            vmem((slabs, 2, 2 * size, 2 * size), BF16),
            vmem((slabs, 2, 2 * size, 2 * size), BF16),
            vmem((slabs, 2 * size, size), F32),
            vmem((slabs, energies, 2, rows, size), F32),
            vmem((2, size, size), F32),
            vmem((slabs, energies, 2, rows, size), F32),
            vmem((2 * size, size), F32),
            vmem((2, 2 * size, size), F32),
            pltpu.SemaphoreType.DMA((4,)),
            pltpu.SemaphoreType.DMA((CHUNKS,)),
            pltpu.SemaphoreType.DMA((CHUNKS,)),
            pltpu.SemaphoreType.DMA((slabs, energies)),
            pltpu.SemaphoreType.DMA((slabs, energies)),
            pltpu.SemaphoreType.DMA((2,)),
            pltpu.SemaphoreType.DMA((2,)),
        ],
        compiler_params=pltpu.CompilerParams(
            collective_id=0, has_side_effects=True
        ),
    )(retain.reshape(slabs), hopping, source, woven)
    greens, self_energy = pl.pallas_call(
        write_out,
        out_shape=(
            jax.ShapeDtypeStruct(source.shape, F32),
            jax.ShapeDtypeStruct(woven.shape, F32),
        ),
        in_specs=[vmem_spec, vmem_spec],
        out_specs=(any_spec, any_spec),
        scratch_shapes=[pltpu.SemaphoreType.DMA((2,))],
        compiler_params=pltpu.CompilerParams(vmem_limit_bytes=4 << 20),
    )(greens, self_energy)
    return greens, (
        self_energy.reshape(slabs, energies, rows, 2, size)
        .transpose(0, 1, 3, 2, 4)
        .reshape(screened.shape)
    )


def solution(mesh):
    placed = (
        P("space", "energy"),
        P("space", "energy", None, None, None),
        P("space", "energy", None, None, None),
        P("space", None, None, "energy"),
    )
    return jax.shard_map(
        body,
        mesh=mesh,
        in_specs=placed,
        out_specs=(P("space", "energy", None, None, None), P("space", None, None, "energy")),
        check_vma=False,
    )
```

```python
import functools

import jax
import jax.numpy as jnp
from jax import lax
from jax.experimental import pallas as pl
from jax.experimental.pallas import tpu as pltpu
from jax.sharding import PartitionSpec as P

MESH = pl.DeviceIdType.MESH
F32 = jnp.float32
BF16 = jnp.bfloat16
CHUNKS = 8
GROUPS = 1
OUTS = 2
NN = (((1,), (0,)), ((), ()))


def split(value):
    high = value.astype(BF16)
    return high, (value - high.astype(F32)).astype(BF16)


def product(left, right, dims=NN):
    dot = functools.partial(lax.dot_general, dimension_numbers=dims, preferred_element_type=F32)
    (lh, ll), (rh, rl) = left, right
    return dot(lh, rh) + (dot(lh, rl) + dot(ll, rh))


def left_form(real, imag):
    return jnp.concatenate(
        [jnp.concatenate([real, -imag], 1), jnp.concatenate([imag, real], 1)], 0
    )


def dagger_form(real, imag):
    real, imag = real.T, imag.T
    return jnp.concatenate(
        [jnp.concatenate([real, -imag], 1), jnp.concatenate([imag, real], 1)], 0
    )


def kernel(
    retain_hbm, hop_hbm, src_hbm, scr_hbm, g, out_se,
    retain, hop, src, scr, lefts, rights, bases, stage, entering, landed, own_map, early,
    load_sem, chain_send, chain_recv, swap_send, swap_recv, early_send, early_recv,
):
    slabs, _, size, _ = hop.shape
    energies, rows = stage.shape[1], stage.shape[3]
    space, energy = lax.axis_index("space"), lax.axis_index("energy")
    stages = lax.axis_size("space")
    piece = size // CHUNKS
    relays = (space % 2 == 0) & (space > 0) & (space < stages - 1)
    paired = (space % 2 == 1) & (space > 1)

    loads = [
        pltpu.make_async_copy(hop_hbm.at[:, 0], hop, load_sem.at[0]),
        pltpu.make_async_copy(src_hbm.at[:, 0], src, load_sem.at[1]),
        pltpu.make_async_copy(scr_hbm, scr, load_sem.at[2]),
        pltpu.make_async_copy(retain_hbm, retain, load_sem.at[3]),
    ]
    for load in loads:
        load.start()

    barrier = pltpu.get_barrier_semaphore()
    for step in range(1, energies):
        pl.semaphore_signal(
            barrier, inc=1, device_id=(space, lax.rem(energy + step, energies)), device_id_type=MESH
        )

    @pl.when(space > 0)
    def _():
        pl.semaphore_signal(barrier, inc=1, device_id=(space - 1, energy), device_id_type=MESH)

    loads[3].wait()
    loads[0].wait()
    loads[1].wait()

    eye = (
        lax.broadcasted_iota(jnp.int32, (size, size), 0)
        == lax.broadcasted_iota(jnp.int32, (size, size), 1)
    ).astype(F32)
    couplers = []
    for j in range(slabs):
        factor = retain[j]
        couplers.append((factor * (eye + hop[j, 0]), factor * hop[j, 1]))

    def sandwich(left, right, real, imag):
        turned = product(split(jnp.concatenate([real, imag], 1)), right)
        return product(left, split(jnp.concatenate([turned[:, :size], turned[:, size:]], 0)))

    base = jnp.concatenate([src[0, 0], src[0, 1]], 0)
    bases[0] = base
    step_lefts = [None]
    for j in range(1, slabs):
        step_left = split(left_form(*couplers[j]))
        step_right = split(dagger_form(*couplers[j]))
        step_lefts.append(step_left)
        base = sandwich(step_left, step_right, base[:size], base[size:]) + jnp.concatenate(
            [src[j, 0], src[j, 1]], 0
        )
        bases[j] = base

    def chain(c, relay=False):
        part = pl.ds(c * piece, piece)
        return pltpu.make_async_remote_copy(
            src_ref=entering.at[:, part] if relay else g.at[slabs - 1, :, part],
            dst_ref=entering.at[:, part],
            send_sem=chain_send.at[c],
            recv_sem=chain_recv.at[c],
            device_id=(space + 1, energy),
            device_id_type=MESH,
        )

    def ahead(i):
        return pltpu.make_async_remote_copy(
            src_ref=bases.at[slabs - 1] if i else own_map,
            dst_ref=early.at[i],
            send_sem=early_send.at[i],
            recv_sem=early_recv.at[i],
            device_id=(space + 1, energy),
            device_id_type=MESH,
        )

    def swap(j, step):
        peer = lax.rem(energy + step, energies)
        return pltpu.make_async_remote_copy(
            src_ref=stage.at[j, peer],
            dst_ref=landed.at[j, energy],
            send_sem=swap_send.at[j, step],
            recv_sem=swap_recv.at[j, step],
            device_id=(space, peer),
            device_id_type=MESH,
        )

    def keep(j, real, imag):
        for ref, form in ((lefts, left_form), (rights, dagger_form)):
            high, low = split(form(real, imag))
            ref[j, 0] = high
            ref[j, 1] = low

    def put(j, block):
        g[j, 0] = block[:size]
        g[j, 1] = block[size:]

    def spread(j):
        for q in range(energies):
            for part in range(2):
                stage[j, q, part] = g[j, part, q * rows : (q + 1) * rows]
        for step in range(1, energies):
            swap(j, step).start()

    pl.semaphore_wait(barrier, energies - 1 + (space < stages - 1).astype(jnp.int32))

    last = slabs - 1

    @pl.when(space == 0)
    def _():
        put(last, bases[last])

        @pl.when(space < stages - 1)
        def _():
            for c in range(CHUNKS):
                chain(c).start()

        spread(last)
        for j in range(last - 1, -1, -1):
            put(j, bases[j])
            spread(j)

    @pl.when(space > 0)
    def _():
        real, imag = couplers[0]
        for j in range(slabs):
            if j > 0:
                both = product(step_lefts[j], split(jnp.concatenate([real, imag], 0)))
                real, imag = both[:size], both[size:]
            keep(j, real, imag)
        own_map[...] = jnp.concatenate([real, imag], 0)

        @pl.when(relays)
        def _():
            ahead(0).start()
            ahead(1).start()

        @pl.when(paired)
        def _():
            ahead(0).wait_recv()
            ahead(1).wait_recv()
            before = split(early[0])
            for j in range(slabs):
                left = lefts[j, 0], lefts[j, 1]
                right = rights[j, 0], rights[j, 1]
                bases[j] = sandwich(left, right, early[1, :size], early[1, size:]) + bases[j]
                both = product(left, before)
                keep(j, both[:size], both[size:])

        turned = []
        for c in range(CHUNKS):
            chain(c).wait_recv()

            @pl.when(relays)
            def _():
                chain(c, True).start()

            if (c + 1) % (CHUNKS // GROUPS) == 0:
                lines = slice((c + 1) * piece - size // GROUPS, (c + 1) * piece)
                arrived = split(jnp.concatenate([entering[0, lines], entering[1, lines]], 1))
                turned.append(product(arrived, (rights[last, 0], rights[last, 1])))
        turned = jnp.concatenate(turned, 0)
        inner = split(jnp.concatenate([turned[:, :size], turned[:, size:]], 0))
        height = size // OUTS
        for o in range(OUTS):
            for part in range(2):
                lines = slice(part * size + o * height, part * size + (o + 1) * height)
                left = lefts[last, 0, lines], lefts[last, 1, lines]
                g[last, part, o * height : (o + 1) * height] = (
                    product(left, inner) + bases[last, lines]
                )

            @pl.when((space < stages - 1) & (space % 2 == 1))
            def _():
                for c in range(o * CHUNKS // OUTS, (o + 1) * CHUNKS // OUTS):
                    chain(c).start()

        spread(last)
        for j in range(last - 1, -1, -1):
            put(
                j,
                sandwich(
                    (lefts[j, 0], lefts[j, 1]),
                    (rights[j, 0], rights[j, 1]),
                    entering[0],
                    entering[1],
                )
                + bases[j],
            )
            spread(j)

    def lanes(part):
        return pl.ds(part, rows, stride=2)

    loads[2].wait()
    for j in range(last, -1, -1):
        landed[j, energy] = stage[j, energy]
        for step in range(1, energies):
            swap(j, step).wait_recv()
        for e in range(energies):
            real = jnp.zeros((rows, size), F32)
            imag = jnp.zeros((rows, size), F32)
            for w in range(e + 1):
                gr, gi = landed[j, e - w, 0], landed[j, e - w, 1]
                sr, si = scr[j, w, lanes(0)], scr[j, w, lanes(1)]
                real = real + (gr * sr - gi * si)
                imag = imag + (gr * si + gi * sr)
            out_se[j, e, lanes(0)] = real
            out_se[j, e, lanes(1)] = imag

    for j in range(slabs):
        for step in range(1, energies):
            swap(j, step).wait_send()

    @pl.when((space < stages - 1) & jnp.logical_not(relays))
    def _():
        for c in range(CHUNKS):
            chain(c).wait_send()

    @pl.when(relays)
    def _():
        ahead(0).wait_send()
        ahead(1).wait_send()
        for c in range(CHUNKS):
            chain(c, True).wait_send()


def write_out(g, se, out_g, out_se, sems):
    copies = [
        pltpu.make_async_copy(g, out_g.at[:, 0], sems.at[0]),
        pltpu.make_async_copy(se, out_se, sems.at[1]),
    ]
    for copy in copies:
        copy.start()
    for copy in copies:
        copy.wait()


def body(retain, hopping, source, screened):
    slabs, _, _, size, _ = hopping.shape
    energies = screened.shape[1]
    rows = screened.shape[3] // size
    woven = (
        screened.reshape(slabs, energies, 2, rows, size)
        .transpose(0, 1, 3, 2, 4)
        .reshape(slabs, energies, 2 * rows, size)
    )
    any_spec = pl.BlockSpec(memory_space=pl.ANY)
    vmem_spec = pl.BlockSpec(memory_space=pltpu.VMEM)
    vmem = pltpu.VMEM
    greens, self_energy = pl.pallas_call(
        kernel,
        out_shape=(vmem((slabs, 2, size, size), F32), vmem(woven.shape, F32)),
        in_specs=[pl.BlockSpec(memory_space=pltpu.HBM)] * 4,
        out_specs=(vmem_spec, vmem_spec),
        scratch_shapes=[
            pltpu.SMEM((slabs,), F32),
            vmem((slabs, 2, size, size), F32),
            vmem((slabs, 2, size, size), F32),
            vmem(woven.shape, F32),
            vmem((slabs, 2, 2 * size, 2 * size), BF16),
            vmem((slabs, 2, 2 * size, 2 * size), BF16),
            vmem((slabs, 2 * size, size), F32),
            vmem((slabs, energies, 2, rows, size), F32),
            vmem((2, size, size), F32),
            vmem((slabs, energies, 2, rows, size), F32),
            vmem((2 * size, size), F32),
            vmem((2, 2 * size, size), F32),
            pltpu.SemaphoreType.DMA((4,)),
            pltpu.SemaphoreType.DMA((CHUNKS,)),
            pltpu.SemaphoreType.DMA((CHUNKS,)),
            pltpu.SemaphoreType.DMA((slabs, energies)),
            pltpu.SemaphoreType.DMA((slabs, energies)),
            pltpu.SemaphoreType.DMA((2,)),
            pltpu.SemaphoreType.DMA((2,)),
        ],
        compiler_params=pltpu.CompilerParams(
            collective_id=0, has_side_effects=True
        ),
    )(retain.reshape(slabs), hopping, source, woven)
    greens, self_energy = pl.pallas_call(
        write_out,
        out_shape=(
            jax.ShapeDtypeStruct(source.shape, F32),
            jax.ShapeDtypeStruct(woven.shape, F32),
        ),
        in_specs=[vmem_spec, vmem_spec],
        out_specs=(any_spec, any_spec),
        scratch_shapes=[pltpu.SemaphoreType.DMA((2,))],
        compiler_params=pltpu.CompilerParams(vmem_limit_bytes=4 << 20),
    )(greens, self_energy)
    return greens, (
        self_energy.reshape(slabs, energies, rows, 2, size)
        .transpose(0, 1, 3, 2, 4)
        .reshape(screened.shape)
    )


def solution(mesh):
    placed = (
        P("space", "energy"),
        P("space", "energy", None, None, None),
        P("space", "energy", None, None, None),
        P("space", None, None, "energy"),
    )
    return jax.shard_map(
        body,
        mesh=mesh,
        in_specs=placed,
        out_specs=(P("space", "energy", None, None, None), P("space", None, None, "energy")),
        check_vma=False,
    )
```

```python
import functools

import jax
import jax.numpy as jnp
from jax import lax
from jax.experimental import pallas as pl
from jax.experimental.pallas import tpu as pltpu
from jax.sharding import PartitionSpec as P

MESH = pl.DeviceIdType.MESH
F32 = jnp.float32
BF16 = jnp.bfloat16
CHUNKS = 8
GROUPS = 1
OUTS = 2
NN = (((1,), (0,)), ((), ()))


def split(value):
    high = value.astype(BF16)
    return high, (value - high.astype(F32)).astype(BF16)


def product(left, right, dims=NN):
    dot = functools.partial(lax.dot_general, dimension_numbers=dims, preferred_element_type=F32)
    (lh, ll), (rh, rl) = left, right
    return dot(jnp.concatenate([lh, lh, ll], 1), jnp.concatenate([rl, rh, rh], 0))


def left_form(real, imag):
    return jnp.concatenate(
        [jnp.concatenate([real, -imag], 1), jnp.concatenate([imag, real], 1)], 0
    )


def dagger_form(real, imag):
    real, imag = real.T, imag.T
    return jnp.concatenate(
        [jnp.concatenate([real, -imag], 1), jnp.concatenate([imag, real], 1)], 0
    )


def round_count(energies):
    return 0


def near_peers(energy, energies):
    if energies:
        return [lax.rem(energy + step, energies) for step in range(1, energies)]
    peers, width = [], 1
    while width < energies:
        peers.append(energy + width * (1 - 2 * ((energy // width) % 2)))
        width *= 2
    return peers


def kernel(
    retain_hbm, hop_hbm, src_hbm, scr_hbm, g, out_se,
    retain, hop, src, scr, lefts, rights, bases, stage, entering, landed, own_map, early,
    load_sem, chain_send, chain_recv, swap_send, swap_recv, early_send, early_recv, ready,
):
    slabs, _, size, _ = hop.shape
    energies, rows = stage.shape[1], stage.shape[3]
    space, energy = lax.axis_index("space"), lax.axis_index("energy")
    stages = lax.axis_size("space")
    piece = size // CHUNKS
    relays = (space % 2 == 0) & (space > 0) & (space < stages - 1)
    paired = (space % 2 == 1) & (space > 1)

    loads = [
        pltpu.make_async_copy(hop_hbm.at[:, 0], hop, load_sem.at[0]),
        pltpu.make_async_copy(src_hbm.at[:, 0], src, load_sem.at[1]),
        pltpu.make_async_copy(scr_hbm, scr, load_sem.at[2]),
        pltpu.make_async_copy(retain_hbm, retain, load_sem.at[3]),
    ]
    for load in loads:
        load.start()

    barrier = pltpu.get_barrier_semaphore()
    near = near_peers(energy, energies)
    for peer in near:
        pl.semaphore_signal(barrier, inc=1, device_id=(space, peer), device_id_type=MESH)

    @pl.when(space > 0)
    def _():
        pl.semaphore_signal(barrier, inc=1, device_id=(space - 1, energy), device_id_type=MESH)

    loads[3].wait()
    loads[0].wait()
    loads[1].wait()

    eye = (
        lax.broadcasted_iota(jnp.int32, (size, size), 0)
        == lax.broadcasted_iota(jnp.int32, (size, size), 1)
    ).astype(F32)
    couplers = []
    for j in range(slabs):
        factor = retain[j]
        couplers.append((factor * (eye + hop[j, 0]), factor * hop[j, 1]))

    def sandwich(left, right, real, imag):
        turned = product(split(jnp.concatenate([real, imag], 1)), right)
        return product(left, split(jnp.concatenate([turned[:, :size], turned[:, size:]], 0)))

    base = jnp.concatenate([src[0, 0], src[0, 1]], 0)
    bases[0] = base
    step_lefts = [None]
    for j in range(1, slabs):
        step_left = split(left_form(*couplers[j]))
        step_right = split(dagger_form(*couplers[j]))
        step_lefts.append(step_left)
        base = sandwich(step_left, step_right, base[:size], base[size:]) + jnp.concatenate(
            [src[j, 0], src[j, 1]], 0
        )
        bases[j] = base

    def chain(c, relay=False):
        part = pl.ds(c * piece, piece)
        return pltpu.make_async_remote_copy(
            src_ref=entering.at[:, part] if relay else g.at[slabs - 1, :, part],
            dst_ref=entering.at[:, part],
            send_sem=chain_send.at[c],
            recv_sem=chain_recv.at[c],
            device_id=(space + 1, energy),
            device_id_type=MESH,
        )

    def ahead(i):
        return pltpu.make_async_remote_copy(
            src_ref=bases.at[slabs - 1] if i else own_map,
            dst_ref=early.at[i],
            send_sem=early_send.at[i],
            recv_sem=early_recv.at[i],
            device_id=(space + 1, energy),
            device_id_type=MESH,
        )

    def swap(j, step):
        peer = lax.rem(energy + step, energies)
        return pltpu.make_async_remote_copy(
            src_ref=stage.at[j, peer],
            dst_ref=landed.at[j, energy],
            send_sem=swap_send.at[j, step],
            recv_sem=swap_recv.at[j, step],
            device_id=(space, peer),
            device_id_type=MESH,
        )

    def keep(j, real, imag):
        for ref, form in ((lefts, left_form), (rights, dagger_form)):
            high, low = split(form(real, imag))
            ref[j, 0] = high
            ref[j, 1] = low

    def put(j, block):
        g[j, 0] = block[:size]
        g[j, 1] = block[size:]

    def spread(j):
        for q in range(energies):
            for part in range(2):
                stage[j, q, part] = g[j, part, q * rows : (q + 1) * rows]
        for step in range(1, energies):
            swap(j, step).start()

    @pl.when(space > 0)
    def _():
        real, imag = couplers[0]
        for j in range(slabs):
            if j > 0:
                both = product(step_lefts[j], split(jnp.concatenate([real, imag], 0)))
                real, imag = both[:size], both[size:]
            keep(j, real, imag)
        own_map[...] = jnp.concatenate([real, imag], 0)

    pl.semaphore_wait(barrier, len(near) + (space < stages - 1).astype(jnp.int32))

    last = slabs - 1

    @pl.when(space == 0)
    def _():
        put(last, bases[last])

        @pl.when(space < stages - 1)
        def _():
            for c in range(CHUNKS):
                chain(c).start()

    @pl.when(relays)
    def _():
        ahead(0).start()
        ahead(1).start()

    for r in range(round_count(energies)):
        for peer in near:
            pl.semaphore_signal(ready.at[r], inc=1, device_id=(space, peer), device_id_type=MESH)
        pl.semaphore_wait(ready.at[r], len(near))

    @pl.when(space == 0)
    def _():
        spread(last)
        for j in range(last - 1, -1, -1):
            put(j, bases[j])
            spread(j)

    @pl.when(space > 0)
    def _():
        @pl.when(paired)
        def _():
            ahead(0).wait_recv()
            ahead(1).wait_recv()
            before = split(early[0])
            for j in range(slabs):
                left = lefts[j, 0], lefts[j, 1]
                right = rights[j, 0], rights[j, 1]
                bases[j] = sandwich(left, right, early[1, :size], early[1, size:]) + bases[j]
                both = product(left, before)
                keep(j, both[:size], both[size:])

        turned = []
        for c in range(CHUNKS):
            chain(c).wait_recv()

            @pl.when(relays)
            def _():
                chain(c, True).start()

            if (c + 1) % (CHUNKS // GROUPS) == 0:
                lines = slice((c + 1) * piece - size // GROUPS, (c + 1) * piece)
                arrived = split(jnp.concatenate([entering[0, lines], entering[1, lines]], 1))
                turned.append(product(arrived, (rights[last, 0], rights[last, 1])))
        turned = jnp.concatenate(turned, 0)
        inner = split(jnp.concatenate([turned[:, :size], turned[:, size:]], 0))
        height = size // OUTS
        for o in range(OUTS):
            for part in range(2):
                lines = slice(part * size + o * height, part * size + (o + 1) * height)
                left = lefts[last, 0, lines], lefts[last, 1, lines]
                g[last, part, o * height : (o + 1) * height] = (
                    product(left, inner) + bases[last, lines]
                )

            @pl.when((space < stages - 1) & (space % 2 == 1))
            def _():
                for c in range(o * CHUNKS // OUTS, (o + 1) * CHUNKS // OUTS):
                    chain(c).start()

        spread(last)
        for j in range(last - 1, -1, -1):
            put(
                j,
                sandwich(
                    (lefts[j, 0], lefts[j, 1]),
                    (rights[j, 0], rights[j, 1]),
                    entering[0],
                    entering[1],
                )
                + bases[j],
            )
            spread(j)

    def lanes(part):
        return pl.ds(part, rows, stride=2)

    loads[2].wait()
    for j in range(last, -1, -1):
        landed[j, energy] = stage[j, energy]
        for step in range(1, energies):
            swap(j, step).wait_recv()
        for e in range(energies):
            real = jnp.zeros((rows, size), F32)
            imag = jnp.zeros((rows, size), F32)
            for w in range(e + 1):
                gr, gi = landed[j, e - w, 0], landed[j, e - w, 1]
                sr, si = scr[j, w, lanes(0)], scr[j, w, lanes(1)]
                real = real + (gr * sr - gi * si)
                imag = imag + (gr * si + gi * sr)
            out_se[j, e, lanes(0)] = real
            out_se[j, e, lanes(1)] = imag

    for j in range(slabs):
        for step in range(1, energies):
            swap(j, step).wait_send()

    @pl.when((space < stages - 1) & jnp.logical_not(relays))
    def _():
        for c in range(CHUNKS):
            chain(c).wait_send()

    @pl.when(relays)
    def _():
        ahead(0).wait_send()
        ahead(1).wait_send()
        for c in range(CHUNKS):
            chain(c, True).wait_send()


def write_out(g, se, out_g, out_se, sems):
    copies = [
        pltpu.make_async_copy(g, out_g.at[:, 0], sems.at[0]),
        pltpu.make_async_copy(se, out_se, sems.at[1]),
    ]
    for copy in copies:
        copy.start()
    for copy in copies:
        copy.wait()


def body(retain, hopping, source, screened):
    slabs, _, _, size, _ = hopping.shape
    energies = screened.shape[1]
    rows = screened.shape[3] // size
    woven = (
        screened.reshape(slabs, energies, 2, rows, size)
        .transpose(0, 1, 3, 2, 4)
        .reshape(slabs, energies, 2 * rows, size)
    )
    any_spec = pl.BlockSpec(memory_space=pl.ANY)
    vmem_spec = pl.BlockSpec(memory_space=pltpu.VMEM)
    vmem = pltpu.VMEM
    greens, self_energy = pl.pallas_call(
        kernel,
        out_shape=(vmem((slabs, 2, size, size), F32), vmem(woven.shape, F32)),
        in_specs=[pl.BlockSpec(memory_space=pltpu.HBM)] * 4,
        out_specs=(vmem_spec, vmem_spec),
        scratch_shapes=[
            pltpu.SMEM((slabs,), F32),
            vmem((slabs, 2, size, size), F32),
            vmem((slabs, 2, size, size), F32),
            vmem(woven.shape, F32),
            vmem((slabs, 2, 2 * size, 2 * size), BF16),
            vmem((slabs, 2, 2 * size, 2 * size), BF16),
            vmem((slabs, 2 * size, size), F32),
            vmem((slabs, energies, 2, rows, size), F32),
            vmem((2, size, size), F32),
            vmem((slabs, energies, 2, rows, size), F32),
            vmem((2 * size, size), F32),
            vmem((2, 2 * size, size), F32),
            pltpu.SemaphoreType.DMA((4,)),
            pltpu.SemaphoreType.DMA((CHUNKS,)),
            pltpu.SemaphoreType.DMA((CHUNKS,)),
            pltpu.SemaphoreType.DMA((slabs, energies)),
            pltpu.SemaphoreType.DMA((slabs, energies)),
            pltpu.SemaphoreType.DMA((2,)),
            pltpu.SemaphoreType.DMA((2,)),
            pltpu.SemaphoreType.REGULAR((max(1, round_count(energies)),)),
        ],
        compiler_params=pltpu.CompilerParams(
            collective_id=0, has_side_effects=True
        ),
    )(retain.reshape(slabs), hopping, source, woven)
    greens, self_energy = pl.pallas_call(
        write_out,
        out_shape=(
            jax.ShapeDtypeStruct(source.shape, F32),
            jax.ShapeDtypeStruct(woven.shape, F32),
        ),
        in_specs=[vmem_spec, vmem_spec],
        out_specs=(any_spec, any_spec),
        scratch_shapes=[pltpu.SemaphoreType.DMA((2,))],
        compiler_params=pltpu.CompilerParams(vmem_limit_bytes=4 << 20),
    )(greens, self_energy)
    return greens, (
        self_energy.reshape(slabs, energies, rows, 2, size)
        .transpose(0, 1, 3, 2, 4)
        .reshape(screened.shape)
    )


def solution(mesh):
    placed = (
        P("space", "energy"),
        P("space", "energy", None, None, None),
        P("space", "energy", None, None, None),
        P("space", None, None, "energy"),
    )
    return jax.shard_map(
        body,
        mesh=mesh,
        in_specs=placed,
        out_specs=(P("space", "energy", None, None, None), P("space", None, None, "energy")),
        check_vma=False,
    )
```
